32 devices in a mesh: groups: 2 (over y), blk: 4 (over z), red: 2 (over x), sub: 2 (over core).
Axes of the slice: x: 2, y: 2, z: 4, core: 2. Of those that a mesh axis runs over, the one named last changes fastest.
Arguments:
- activations: bfloat16 [2, 16, 128, 8192], P('red', ('groups', 'blk', 'sub')), parts along dimension 1, may hold values from -6 to 6
- out_grads: bfloat16 [2, 16, 128, 8192], P('red', ('groups', 'blk', 'sub')), parts along dimension 1, may hold values from -6 to 6
- lengths: int32 [2, 16], P('red', ('groups', 'blk', 'sub')), parts along dimension 1, may hold values from 32 to 128
- proj_in: bfloat16 [8192, 256], P(('blk', 'red', 'sub')), may hold values from -0.0625 to 0.0625
- proj_out: bfloat16 [8192, 256], P(('blk', 'red', 'sub')), may hold values from -0.0625 to 0.0625
- queries: bfloat16 [512, 256, 256], P(('groups', 'red'), ('blk', 'sub')), parts along dimension 0, may hold values from -6 to 6
Outputs:
- scores: float32 [512, 16], P(('groups', 'blk', 'sub'), 'red'), parts along dimension 0
The draws below stay inside these ranges and needn't reach their ends.
There are 2 independent parts, one for each index of `groups`. The reference program is written for one: setup_inputs(seed, part) draws one part's arguments, and reference() takes and returns one part's arrays. A program takes and returns all parts, laid end to end along the dimension named above; an argument that names none is the same for every part. Nothing has to cross between parts.
All inputs are finite; a program needn't handle non-finite values.
Results may differ from the reference program's by a relative error of at most 0.0051.
Values may be sent and summed in bfloat16 or wider, within the bound.
No kernel may reach another device: no remote copies, remote signals or barrier semaphores. Data moves between devices by JAX's collectives and lax.ppermute only.
A program may use at most 128 MiB of HBM per device.

```python
import math
import jax
import jax.numpy as jnp
from jax import lax

D = 8192
R = 256
BS = 512
LEN = 128
Q = 256
NS_STEPS = 2
BLOCKS = 128
GROUP_EX = 8
EXAMPLES = 16
N_RED = 2


def set_ends(array, own_key, low, high):
    index_at = [jax.random.randint(jax.random.fold_in(own_key, axis), (), 0, length) for axis, length in enumerate(array.shape)]
    widest = array.shape.index(max(array.shape))
    next_to = index_at[:widest] + [(index_at[widest] + 1) % array.shape[widest]] + index_at[widest + 1:]
    return array.at[tuple(index_at)].set(low).at[tuple(next_to)].set(high)


def steps_of(own_key, dims, cuts, least, top_value):
    def one(position, parts):
        heights = jax.random.uniform(jax.random.fold_in(jax.random.fold_in(own_key, 6), position), (parts,), jnp.float32, least / len(cuts), top_value / len(cuts))
        return jnp.repeat(jnp.exp(heights), dims[position] // parts).reshape((-1,) + (1,) * (len(dims) - position - 1))

    level = one(*cuts[0])
    for cut in cuts[1:]:
        level = level * one(*cut)
    return level


def gaussian(rng, shape, deviation, reach, cuts=(), kind=jnp.bfloat16):
    values = deviation * jax.random.normal(rng, shape, jnp.float32)
    if cuts:
        values = values * steps_of(rng, shape, cuts, -0.22, 0.18)
    return jnp.clip(values, -reach, reach).astype(kind)


def setup_inputs(seed: int = 0, part: int = 0) -> dict:
    key_of = jax.random.split(jax.random.key(seed), 7)
    own_keys = jax.random.split(jax.random.fold_in(key_of[6], part), 7)
    return {
        "activations": gaussian(own_keys[0], (N_RED, GROUP_EX, LEN, D), 1.0, 6.0, ((0, 2), (1, 8))),
        "out_grads": gaussian(own_keys[1], (N_RED, GROUP_EX, LEN, D), 1.0, 6.0, ((0, 2), (1, 8))),
        "lengths": set_ends(jax.random.randint(own_keys[2], (N_RED, GROUP_EX), LEN // 4, LEN + 1), jax.random.fold_in(own_keys[2], 1), LEN // 4, LEN).astype(jnp.int32),
        "proj_in": gaussian(key_of[3], (D, R), D ** -0.5, 0.0625, ((0, 16),)),
        "proj_out": gaussian(key_of[4], (D, R), D ** -0.5, 0.0625, ((0, 16),)),
        "queries": gaussian(own_keys[5], (Q, R, R), 1.0, 6.0, ((0, 2), (1, 8))),
    }


DAMPING = 0.1
HIGH = lax.Precision.HIGHEST

def reference(activations, out_grads, lengths, proj_in, proj_out, queries):
    tokens_all = activations.reshape(EXAMPLES, LEN, D)
    grads_all = out_grads.reshape(EXAMPLES, LEN, D)
    length_all = lengths.reshape(EXAMPLES)

    def project(item):
        tokens_one, grads_one, length_one = item
        live_mask = jnp.arange(LEN, dtype=jnp.int32)[:, None] < length_one
        masked = jnp.where(live_mask, grads_one, jnp.zeros((), grads_one.dtype))
        in_side = jnp.dot(tokens_one, proj_in, preferred_element_type=jnp.float32).astype(jnp.bfloat16)
        out_side = jnp.dot(masked, proj_out, preferred_element_type=jnp.float32).astype(jnp.bfloat16)
        return jnp.dot(out_side.T, in_side, preferred_element_type=jnp.float32).astype(jnp.bfloat16)
    projected = lax.map(project, (tokens_all, grads_all, length_all))
    coords = projected.reshape(EXAMPLES, BLOCKS, BS).astype(jnp.float32)
    fisher = jnp.einsum('ekc,ekd->kcd', coords, coords, precision=HIGH) / EXAMPLES
    ident = jnp.eye(BS, dtype=jnp.float32)
    trace = lax.optimization_barrier(jnp.sum(fisher * ident, axis=(1, 2)))
    damping = DAMPING * trace / BS
    hessian = fisher + damping[:, None, None] * ident
    scale = lax.rsqrt(lax.optimization_barrier(jnp.sum(hessian * hessian, axis=(1, 2))))[:, None, None]
    inverse = scale * (2.0 * ident - scale * hessian)
    for sweep in range(NS_STEPS):
        image = jnp.einsum('kab,kbc->kac', hessian, inverse, precision=HIGH)
        inverse = jnp.einsum('kab,kbc->kac', inverse, 2.0 * ident - image, precision=HIGH)
    query_coords = queries.reshape(Q, BLOCKS, BS).astype(jnp.float32)
    weighted = jnp.einsum('kcd,qkd->kcq', inverse, query_coords, precision=HIGH)
    scores = jnp.einsum('kcq,ekc->qe', weighted, coords, precision=HIGH)
    return scores * (1.0 / math.sqrt(BLOCKS))
```

```python
import functools
import math

import jax
import jax.numpy as jnp
from jax import lax
from jax.experimental import pallas as pl
from jax.experimental.pallas import tpu as pltpu
from jax.sharding import PartitionSpec as P

BS = 512
NS_STEPS = 2
DAMPING = 0.1
HIGH = lax.Precision.HIGHEST
ALL = ("blk", "red", "sub")


def shift(value, axis, by):
    size = lax.axis_size(axis)
    return lax.ppermute(value, axis, [(i, (i + by) % size) for i in range(size)])


def gather_pieces(first, second):
    n_blk, n_red, n_groups = (lax.axis_size(a) for a in ("blk", "red", "groups"))
    if n_groups == 2:
        group = lax.axis_index("groups")
        mine = jnp.where(group == 0, first, second)
        other = jnp.where(group == 0, second, first)
    else:
        mine, other = first, second

    def across(value, fallback):
        return shift(value, "groups", 1) if n_groups == 2 else fallback()

    up = (n_blk - 1) - (n_blk - 1) // 2
    down = (n_blk - 1) // 2
    m = {(0, 0): mine}
    o = {(0, 0): other}
    for d in range(1, up + 1):
        m[d, 0] = shift(m[d - 1, 0], "blk", 1)
        if d <= down:
            m[-d, 0] = shift(m[1 - d, 0], "blk", -1)
    order = sorted({d for d, _ in m}, key=lambda d: (abs(d), -d))
    for d in order:
        for j in range(1, n_red):
            m[d, j] = shift(m[d, j - 1], "red", 1)
    for d in order:
        if d == 1:
            o[d, 0] = across(m[d, 0], lambda: shift(other, "blk", 1))
        elif d:
            step = 1 if d > 0 else -1
            o[d, 0] = shift(o[d - step, 0], "blk", step)
        for j in range(1, n_red):
            if d == 0:
                o[d, j] = shift(o[d, j - 1], "red", 1)
            else:
                o[d, j] = across(m[d, j], lambda: shift(o[d, j - 1], "red", 1))
    return [(d, j, m[d, j], o[d, j]) for d in order for j in range(n_red)]


def solve_kernel(n_blk, n_red, n_sub, per_block, coords_ref, queries_ref, out_ref):
    examples, per_dev, width = coords_ref.shape
    n_q = queries_ref.shape[1]
    blocks = per_dev // per_block
    side = blocks * examples
    flat = coords_ref[...].reshape(examples * per_dev, width)

    row = lax.broadcasted_iota(jnp.int32, (side, examples * per_dev), 0)
    col = lax.broadcasted_iota(jnp.int32, (side, examples * per_dev), 1)
    block, slot = row // examples, row % examples
    red, rest = slot // (n_blk * n_sub), slot % (n_blk * n_sub)
    source = ((rest // n_sub) * n_red + red) * n_sub + rest % n_sub
    start = source * per_dev + block * per_block
    parts = []
    for j in range(per_block):
        pick = (col == start + j).astype(jnp.float32).astype(jnp.bfloat16)
        parts.append(jnp.dot(pick, flat, preferred_element_type=jnp.float32).astype(jnp.bfloat16))

    contract = (((1,), (1,)), ((), ()))
    gram = jnp.zeros((side, side), jnp.float32)
    for part in parts:
        gram += lax.dot_general(part, part, contract, preferred_element_type=jnp.float32)
    rows = lax.broadcasted_iota(jnp.int32, (side, side), 0)
    cols = lax.broadcasted_iota(jnp.int32, (side, side), 1)
    same = (rows // examples) == (cols // examples)
    ident = (rows == cols).astype(jnp.float32)
    fisher = jnp.where(same, gram, 0.0) * (1.0 / examples)

    def per_block_sum(values):
        column = jnp.sum(values, axis=0, keepdims=True)
        return jnp.sum(jnp.where(same, column, 0.0), axis=1, keepdims=True)

    trace = per_block_sum(fisher * ident)
    damping = DAMPING * trace / BS
    total = per_block_sum(fisher * fisher) + 2.0 * damping * trace + BS * (damping * damping)
    scale = lax.rsqrt(total)
    hessian = fisher + damping * ident
    inverse = scale * (2.0 * ident - scale * hessian)
    inverse = jnp.where(same, inverse, 0.0)
    for _ in range(NS_STEPS):
        image = jnp.dot(hessian, inverse, precision=HIGH, preferred_element_type=jnp.float32)
        inverse = jnp.dot(inverse, 2.0 * ident - image, precision=HIGH, preferred_element_type=jnp.float32)

    products = []
    for k in range(blocks):
        total_k = jnp.zeros((examples, n_q), jnp.float32)
        for j in range(per_block):
            total_k += lax.dot_general(
                parts[j][k * examples:(k + 1) * examples],
                queries_ref[k * per_block + j],
                contract,
                preferred_element_type=jnp.float32,
            )
        products.append(total_k)
    images = jnp.concatenate(products, axis=0)
    weighted = jnp.dot(inverse, images, precision=HIGH, preferred_element_type=jnp.float32)
    scores = weighted[:examples]
    for k in range(1, blocks):
        scores += weighted[k * examples:(k + 1) * examples]
    out_ref[...] = scores


def partial_scores(coords, queries, sizes, per_block):
    examples = coords.shape[0]
    n_q = queries.shape[1]
    return pl.pallas_call(
        functools.partial(solve_kernel, *sizes, per_block),
        out_shape=jax.ShapeDtypeStruct((examples, n_q), jnp.float32),
        in_specs=[pl.BlockSpec(memory_space=pltpu.VMEM)] * 2,
        out_specs=pl.BlockSpec(memory_space=pltpu.VMEM),
        compiler_params=pltpu.CompilerParams(vmem_limit_bytes=32 * 1024 * 1024),
    )(coords, queries)


def on_device(activations, out_grads, lengths, proj_in, proj_out, queries):
    sizes = n_blk, n_red, n_sub = tuple(lax.axis_size(a) for a in ALL)
    i_blk, i_red, i_sub = (lax.axis_index(a) for a in ALL)
    seq_len, width = activations.shape[2:]
    depth, rank_in = proj_in.shape
    rank_out = proj_out.shape[1]
    units = width // (depth * n_sub)
    per_block = BS // rank_in

    def columns(array, core):
        split = array.reshape(seq_len, units, n_sub, depth)
        return lax.dynamic_index_in_dim(split, core, axis=2, keepdims=False).reshape(seq_len, units * depth)

    def spread(array):
        held = [columns(array, i_sub)]
        for step in range(1, n_sub):
            held.append(shift(columns(array, (i_sub + step) % n_sub), "sub", step))
        return jnp.concatenate(held, axis=0)

    tokens, grads = spread(activations), spread(out_grads)
    queries_by_row = jnp.transpose(queries, (1, 0, 2))

    group = lax.axis_index("groups")
    swapped = lax.axis_size("groups") == 2
    sums = [jnp.zeros((n_sub * seq_len, rank_in), jnp.float32), jnp.zeros((n_sub * seq_len, rank_out), jnp.float32)]
    if swapped:
        lefts = [jnp.where(group == 0, tokens, grads), jnp.where(group == 0, grads, tokens)]
    else:
        lefts = [tokens, grads]
    for d, j, one, two in gather_pieces(proj_in, proj_out):
        unit = ((i_blk - d) % n_blk) * n_red + (i_red - j) % n_red
        for i, piece in enumerate((one, two)):
            left = lax.dynamic_slice_in_dim(lefts[i], unit * depth, depth, axis=1)
            sums[i] += jnp.dot(left, piece, preferred_element_type=jnp.float32)
    if swapped:
        sums = [jnp.where(group == 0, sums[0], sums[1]), jnp.where(group == 0, sums[1], sums[0])]

    def own(total):
        kept = total[:seq_len]
        for step in range(1, n_sub):
            kept += shift(total[step * seq_len:(step + 1) * seq_len], "sub", -step)
        return kept

    in_side = own(sums[0]).astype(jnp.bfloat16)
    live = lax.broadcasted_iota(jnp.int32, (seq_len, 1), 0) < lengths
    out_side = jnp.where(live, own(sums[1]), 0.0).astype(jnp.bfloat16)
    projected = lax.dot_general(
        out_side, in_side, (((0,), (0,)), ((), ())), preferred_element_type=jnp.float32
    ).astype(jnp.bfloat16)

    rows = rank_out // (n_blk * n_sub)
    sent = jnp.broadcast_to(
        projected.reshape(n_blk, 1, n_sub, rows, rank_in), (n_blk, n_red, n_sub, rows, rank_in)
    ).reshape(n_blk * n_red * n_sub, rows, rank_in)
    coords = lax.all_to_all(sent, ALL, split_axis=0, concat_axis=0, tiled=True)

    part = partial_scores(coords, queries_by_row, sizes, per_block)
    examples, n_q = part.shape
    held = examples // n_red
    sent = jnp.broadcast_to(
        part.reshape(1, n_red, 1, held, n_q), (n_blk, n_red, n_sub, held, n_q)
    ).reshape(n_blk * n_red * n_sub, held, n_q)
    back = lax.all_to_all(sent, ALL, split_axis=0, concat_axis=0, tiled=True)
    back = back.reshape(n_blk, n_red, n_sub, held, n_q)
    chunk = n_q * n_red // (n_blk * n_sub)
    chunks = n_q // chunk
    place = i_blk * n_sub + i_sub
    mine = lax.dynamic_index_in_dim(back, place // chunks, axis=1, keepdims=False)
    scores = jnp.sum(mine, axis=(0, 1))
    scores = lax.dynamic_slice_in_dim(scores, (place % chunks) * chunk, chunk, axis=1)
    blocks = rank_in * rank_out // BS
    return scores.T * (1.0 / math.sqrt(blocks))


def solution(mesh):
    placed = (
        P("red", ("groups", "blk", "sub"), None, None),
        P("red", ("groups", "blk", "sub"), None, None),
        P("red", ("groups", "blk", "sub")),
        P(("blk", "red", "sub"), None),
        P(("blk", "red", "sub"), None),
        P(("groups", "red"), ("blk", "sub"), None),
    )
    return jax.shard_map(
        on_device,
        mesh=mesh,
        in_specs=placed,
        out_specs=P(("groups", "blk", "sub"), "red"),
        check_vma=False,
    )
```
